32 devices in a mesh: dp: 8 (over y, x, core), tensor: 4 (over z).
Axes of the slice: x: 2, y: 2, z: 4, core: 2. Of those that a mesh axis runs over, the one named last changes fastest.
Arguments:
- tokens: bfloat16 [16384, 640], P(('dp', 'tensor')), may hold values from -6 to 6
- segments: int32 [16384], P('dp'), may hold values from 0 to 10, as said below
- positions: int32 [16384], P('dp'), may hold values from 0 to 1999, as said below
- norm_gains: bfloat16 [4, 640], P(None, 'dp'), may hold values from 0.099609375 to 1.8984375
- qk_gains: bfloat16 [2, 256], P(None, 'dp'), may hold values from 0.099609375 to 1.8984375
- q_weight: bfloat16 [640, 1024], P('dp', 'tensor'), may hold values from -0.25 to 0.25
- kv_weight: bfloat16 [640, 512], P('dp'), may hold values from -0.25 to 0.25
- out_weight: bfloat16 [1024, 640], P('tensor', 'dp'), may hold values from -0.1875 to 0.1875
- gate_weight: bfloat16 [640, 2048], P('dp', 'tensor'), may hold values from -0.25 to 0.25
- up_weight: bfloat16 [640, 2048], P('dp', 'tensor'), may hold values from -0.25 to 0.25
- down_weight: bfloat16 [2048, 640], P('tensor', 'dp'), may hold values from -0.125 to 0.125
- cotangent: bfloat16 [16384, 640], P(('dp', 'tensor')), may hold values from -6 to 6
Outputs:
- block_out: bfloat16 [16384, 640], P(('dp', 'tensor'))
- tokens_grad: float32 [16384, 640], P(('dp', 'tensor'))
- norm_gains_grad: float32 [4, 640], P(None, 'dp')
- qk_gains_grad: float32 [2, 256], P(None, 'dp')
- q_weight_grad: float32 [640, 1024], P('dp', 'tensor')
- kv_weight_grad: float32 [640, 512], P('dp')
- out_weight_grad: float32 [1024, 640], P('tensor', 'dp')
- gate_weight_grad: float32 [640, 2048], P('dp', 'tensor')
- up_weight_grad: float32 [640, 2048], P('dp', 'tensor')
- down_weight_grad: float32 [2048, 640], P('tensor', 'dp')
The draws below stay inside these ranges and needn't reach their ends.
Inputs may be any that keep to these rules, and one draw needn't show every extreme that they name: `segments`: within each sequence of 2048 tokens the segment numbers start at 0 and rise by one at each new document; every document except the last of its sequence holds between 200 and 2000 tokens. `positions`: each token's place within its document, 0 at the document's first token.
All inputs are finite; a program needn't handle non-finite values.
Results may differ from the reference program's by a relative error of at most 0.018.
Values may be sent and summed in bfloat16 or wider, within the bound.
A program may use at most 128 MiB of HBM per device.

```python
import jax
import jax.numpy as jnp
from jax import lax

D = 640
HEADS = 4
HD = 256
FF = 2048
WINDOW = 512
LEN = 2048
TOKENS = 16384


def doc_layout(key):
    seq_count = TOKENS // LEN
    shortest = LEN * 25 // 256
    longest = LEN * 125 // 128
    lengths = jax.random.randint(jax.random.fold_in(key, 11), (seq_count, 16), shortest, longest + 1, dtype=jnp.int32)
    lengths = lengths.at[0, 0].set(longest)
    lengths = lengths.at[seq_count - 1].set(jnp.full((16,), shortest, jnp.int32))
    ends = jnp.cumsum(lengths, axis=1).astype(jnp.int32)
    places = jnp.arange(LEN, dtype=jnp.int32)
    doc_ids = jnp.sum((ends[:, None, :] <= places[None, :, None]).astype(jnp.int32), axis=2).astype(jnp.int32)
    starts = jnp.concatenate([jnp.zeros((seq_count, 1), jnp.int32), ends[:, :-1]], axis=1)
    inside = places[None, :] - jnp.take_along_axis(starts, doc_ids, axis=1)
    return (doc_ids.reshape(-1).astype(jnp.int32), inside.reshape(-1).astype(jnp.int32))


def draw_segments(key, part):
    return doc_layout(key)[0]


def draw_positions(key, part):
    return doc_layout(key)[1]


def spiked(drawn, stream_key, source, target, parts, factor):
    def block_of(dim):
        return (jnp.arange(drawn.shape[dim]) // (drawn.shape[dim] // parts)).reshape((-1,) + (1,) * (drawn.ndim - 1 - dim))

    first = jax.random.permutation(stream_key, parts)[block_of(target)]
    other_side = (block_of(target) + parts // 2) % parts
    return jnp.where((block_of(source) == first) | (block_of(source) == other_side), factor * drawn, drawn)


def block_scale(rng, shape, pieces, smallest, high):
    loudness = 1.0
    for axis_at, blocks in pieces:
        steps = jax.random.uniform(jax.random.fold_in(jax.random.fold_in(rng, 6), axis_at), (blocks,), jnp.float32, smallest / len(pieces), high / len(pieces))
        loudness = loudness * jnp.repeat(jnp.exp(steps), shape[axis_at] // blocks).reshape((-1,) + (1,) * (len(shape) - 1 - axis_at))
    return loudness


def scatter_about(stream_key, dims, deviation, reach, cuts=(), kind=jnp.bfloat16):
    result = deviation * jax.random.normal(stream_key, dims, jnp.float32)
    if cuts:
        result = result * block_scale(stream_key, dims, cuts, -0.22, 0.18)
    return jnp.clip(result, -reach, reach).astype(kind)


def heavy_noise(rng, shape, scale, bound, pieces, heavy, held_as=jnp.bfloat16):
    values = scale * jax.random.normal(rng, shape, jnp.float32)
    if pieces:
        values = values * block_scale(rng, shape, pieces, -0.22, 0.18)
    return jnp.clip(spiked(values, jax.random.fold_in(rng, 3), *heavy), -bound, bound).astype(held_as)


def setup_inputs(seed: int = 0) -> dict:
    keys = jax.random.split(jax.random.key(seed), 13)
    return {
        "tokens": heavy_noise(keys[0], (TOKENS, D), 1.0, 6.0, ((0, 32),), (0, 1, 32, 2.75)),
        "segments": draw_segments(jax.random.fold_in(keys[12], 71), 0),
        "positions": draw_positions(jax.random.fold_in(keys[12], 71), 0),
        "norm_gains": jnp.clip(1.0 + 0.18 * jax.random.normal(keys[3], (4, D), jnp.float32), 0.099609375, 1.8984375).astype(jnp.bfloat16),
        "qk_gains": jnp.clip(1.0 + 0.18 * jax.random.normal(keys[4], (2, HD), jnp.float32), 0.099609375, 1.8984375).astype(jnp.bfloat16),
        "q_weight": scatter_about(keys[5], (D, HEADS * HD), D ** -0.5, 0.25, ((0, 8), (1, 4))),
        "kv_weight": scatter_about(keys[6], (D, 2 * HD), D ** -0.5, 0.25, ((0, 8),)),
        "out_weight": scatter_about(keys[7], (HEADS * HD, D), (HEADS * HD) ** -0.5, 0.1875, ((0, 4), (1, 8))),
        "gate_weight": scatter_about(keys[8], (D, FF), D ** -0.5, 0.25, ((0, 8), (1, 4))),
        "up_weight": scatter_about(keys[9], (D, FF), D ** -0.5, 0.25, ((0, 8), (1, 4))),
        "down_weight": scatter_about(keys[10], (FF, D), FF ** -0.5, 0.125, ((0, 4), (1, 8))),
        "cotangent": heavy_noise(keys[11], (TOKENS, D), 1.0, 6.0, ((0, 32),), (0, 1, 32, 2.75)),
    }


EPSILON = 1e-06
ROPE_BASE = 10000.0
GELU_SCALE = 0.7978845608028654
HIGHEST = lax.Precision.HIGHEST

@jax.custom_vjp
def low(v):
    return lax.optimization_barrier(v.astype(jnp.bfloat16)).astype(jnp.float32)

@jax.custom_vjp
def low_back(v):
    return v

def low_keep(v):
    return (low(v), None)

def low_pass(kept, grad):
    return (grad,)

def back_keep(v):
    return (v, None)

def back_low(kept, grad):
    return (low(grad),)
low.defvjp(low_keep, low_pass)
low_back.defvjp(back_keep, back_low)

def norm_rows(values, gain_row):
    return values * lax.rsqrt(lax.optimization_barrier(jnp.mean(values * values, axis=-1, keepdims=True)) + EPSILON) * gain_row

def rotate(values, cosine_table, sine_table):
    half_width = values.shape[-1] // 2
    first_half = values[..., :half_width]
    second_half = values[..., half_width:]
    return jnp.concatenate([first_half * cosine_table - second_half * sine_table, second_half * cosine_table + first_half * sine_table], axis=-1)

def geglu(gate_pre, up_pre):
    inner_term = GELU_SCALE * (gate_pre + 0.044715 * gate_pre * gate_pre * gate_pre)
    return 0.5 * gate_pre * (1.0 + jnp.tanh(inner_term)) * up_pre

def product(left_side, right_side):
    return jnp.dot(left_side, right_side, precision=HIGHEST, preferred_element_type=jnp.float32)

def key_blocks(values, window_rows, fill_value):
    padding = jnp.full((window_rows,) + values.shape[1:], fill_value, values.dtype)
    padded = jnp.concatenate([padding, values], axis=0)
    block_count = values.shape[0] // window_rows
    block_shape = (block_count, window_rows) + values.shape[1:]
    return jnp.concatenate([padded[:-window_rows].reshape(block_shape), padded[window_rows:].reshape(block_shape)], axis=1)

def forward(inputs, norm_gains, qk_gains, q_weight, kv_weight, out_weight, gate_weight, up_weight, down_weight, doc_keys, place_rows):
    span = inputs.shape[0]
    head_width = qk_gains.shape[1]
    head_count = q_weight.shape[1] // head_width
    normed = low(norm_rows(inputs, norm_gains[0]))
    query_raw = low_back(product(normed, q_weight)).reshape(span, head_count, head_width)
    kv_raw = product(normed, kv_weight)
    half_width = head_width // 2
    frequency = ROPE_BASE ** (-jnp.arange(half_width, dtype=jnp.float32) * 2.0 / head_width)
    angles = place_rows.astype(jnp.float32)[:, None] * frequency[None, :]
    cosine_table = jnp.cos(angles)
    sine_table = jnp.sin(angles)
    queries = low(rotate(norm_rows(query_raw, qk_gains[0]), cosine_table[:, None, :], sine_table[:, None, :]))
    key_list = []
    value_list = []
    for head in range(head_count):
        kv_copy = low_back(kv_raw)
        key_list.append(low(rotate(norm_rows(kv_copy[:, :head_width], qk_gains[1]), cosine_table, sine_table)))
        value_list.append(low(kv_copy[:, head_width:]))
    key_rows = jnp.stack(key_list, axis=1)
    value_rows = jnp.stack(value_list, axis=1)
    block_count = span // WINDOW
    query_blocks = queries.reshape(block_count, WINDOW, head_count, head_width)
    key_parts = key_blocks(key_rows, WINDOW, 0.0)
    value_parts = key_blocks(value_rows, WINDOW, 0.0)
    query_docs = doc_keys.reshape(block_count, WINDOW)
    key_docs = key_blocks(doc_keys, WINDOW, -1)
    offsets = jnp.arange(WINDOW)[:, None] + WINDOW - jnp.arange(2 * WINDOW)[None, :]
    near_mask = (offsets >= 0) & (offsets < WINDOW)
    score_scale = head_width ** (-0.5)

    def attend(block_item):
        query_part, key_part, value_part, doc_query, doc_key = block_item
        raw_scores = low_back(jnp.einsum('qhd,khd->hqk', query_part, key_part, precision=HIGHEST)) * score_scale
        allowed = near_mask & (doc_query[:, None] == doc_key[None, :])
        masked = jnp.where(allowed[None], raw_scores, -1000000000.0)
        row_max = lax.optimization_barrier(jnp.max(masked, axis=2, keepdims=True))
        exponent = jnp.exp(masked - row_max)
        probabilities = low(exponent / lax.optimization_barrier(jnp.sum(exponent, axis=2, keepdims=True)))
        return jnp.einsum('hqk,khd->qhd', probabilities, value_part, precision=HIGHEST)
    context = lax.map(jax.checkpoint(attend), (query_blocks, key_parts, value_parts, query_docs, key_docs))
    context = low(low_back(context.reshape(span, head_count * head_width)))
    attn = low_back(product(context, out_weight))
    residual = inputs + norm_rows(attn, norm_gains[1])
    ffn_in = low(norm_rows(residual, norm_gains[2]))
    gate_pre = low_back(product(ffn_in, gate_weight))
    up_pre = low_back(product(ffn_in, up_weight))
    hidden = low(geglu(gate_pre, up_pre))
    ffn = low_back(product(hidden, down_weight))
    return residual + norm_rows(ffn, norm_gains[3])

def reference(tokens, segments, positions, norm_gains, qk_gains, q_weight, kv_weight, out_weight, gate_weight, up_weight, down_weight, cotangent):
    weights = (norm_gains.astype(jnp.float32), qk_gains.astype(jnp.float32), q_weight.astype(jnp.float32), kv_weight.astype(jnp.float32), out_weight.astype(jnp.float32), gate_weight.astype(jnp.float32), up_weight.astype(jnp.float32), down_weight.astype(jnp.float32))
    seq_count = tokens.shape[0] // LEN
    width_all = tokens.shape[1]
    input_seqs = tokens.astype(jnp.float32).reshape(seq_count, LEN, width_all)
    grad_seqs = cotangent.astype(jnp.float32).reshape(seq_count, LEN, width_all)
    doc_seqs = segments.reshape(seq_count, LEN)
    place_seqs = positions.reshape(seq_count, LEN)

    def one_sequence(carry, item):
        inputs, grad_out, doc_keys, place_rows = item

        def layer(inputs, *params):
            return forward(inputs, *params, doc_keys, place_rows)
        outputs, backward = jax.vjp(layer, inputs, *weights)
        grads = backward(grad_out)
        carry = tuple((total + piece for total, piece in zip(carry, grads[1:])))
        return (carry, (outputs.astype(jnp.bfloat16), grads[0]))
    start_sums = tuple((jnp.zeros(w.shape, jnp.float32) for w in weights))
    sums, (output_seqs, input_grads) = lax.scan(one_sequence, start_sums, (input_seqs, grad_seqs, doc_seqs, place_seqs))
    block_out = output_seqs.reshape(seq_count * LEN, width_all)
    tokens_grad = input_grads.reshape(seq_count * LEN, width_all)
    return (block_out, tokens_grad, sums[0], sums[1], sums[2], sums[3], sums[4], sums[5], sums[6], sums[7])
```

```python
import jax
import jax.numpy as jnp
from jax import lax
from jax.sharding import PartitionSpec as P

WINDOW = 512
GAIN_COLUMNS = 128


EPSILON = 1e-06
ROPE_BASE = 10000.0
GELU_SCALE = 0.7978845608028654


def norm_rows(values, gain_row):
    return (
        values * lax.rsqrt(jnp.mean(values * values, axis=-1, keepdims=True) + EPSILON) * gain_row
    )


def norm_back(values, gain_row, grad_out):
    inv_rms = lax.rsqrt(jnp.mean(values * values, axis=-1, keepdims=True) + EPSILON)
    weighted = grad_out * gain_row
    inner_mean = jnp.mean(values * weighted, axis=-1, keepdims=True)
    return (
        inv_rms * weighted - values * inv_rms * inv_rms * inv_rms * inner_mean,
        grad_out * values * inv_rms,
    )


def rotate(values, cosine_table, sine_table):
    half_width = values.shape[-1] // 2
    first_half = values[..., :half_width]
    second_half = values[..., half_width:]
    return jnp.concatenate(
        [
            first_half * cosine_table - second_half * sine_table,
            second_half * cosine_table + first_half * sine_table,
        ],
        axis=-1,
    )


def geglu(gate_pre, up_pre):
    inner_term = GELU_SCALE * (gate_pre + 0.044715 * gate_pre * gate_pre * gate_pre)
    return 0.5 * gate_pre * (1.0 + jnp.tanh(inner_term)) * up_pre


def dot_plain(left_side, right_side):
    return jnp.dot(left_side, right_side, preferred_element_type=jnp.float32)


def dot_last(left_side, right_side):
    return lax.dot_general(
        left_side, right_side, (((1,), (1,)), ((), ())), preferred_element_type=jnp.float32
    )


def dot_first(left_side, right_side):
    return lax.dot_general(
        left_side, right_side, (((0,), (0,)), ((), ())), preferred_element_type=jnp.float32
    )


def pack_shards(norm_gains, qk_gains, q_weight, kv_weight, out_weight, gate_weight, up_weight, down_weight):
    rows = q_weight.shape[0]
    kv_columns = kv_weight.shape[1] // lax.axis_size("tensor")
    kv_part = lax.dynamic_slice_in_dim(
        kv_weight, lax.axis_index("tensor") * kv_columns, kv_columns, axis=1
    )
    gain_part = jnp.concatenate(
        [
            norm_gains.T,
            jnp.pad(qk_gains.T, ((0, rows - qk_gains.shape[1]), (0, 0))),
            jnp.zeros((rows, GAIN_COLUMNS - 6), jnp.bfloat16),
        ],
        axis=1,
    )
    return jnp.concatenate(
        [q_weight, out_weight.T, gate_weight, up_weight, down_weight.T, kv_part, gain_part],
        axis=1,
    )


def gather_weights(packed):
    return lax.all_gather(packed, ("tensor", "dp"), axis=0, tiled=True)


def reduce_grads(grads):
    return lax.psum_scatter(
        grads, ("tensor", "dp"), scatter_dimension=0, tiled=True
    ).astype(jnp.float32)


def per_device(
    tokens,
    segments,
    positions,
    norm_gains,
    qk_gains,
    q_weight,
    kv_weight,
    out_weight,
    gate_weight,
    up_weight,
    down_weight,
    cotangent,
):
    parts = lax.axis_size("tensor")
    place = lax.axis_index("tensor")
    rows, width = tokens.shape
    shard_rows = q_weight.shape[0]
    head_width = q_weight.shape[1]
    ff_part = gate_weight.shape[1]
    kv_columns = kv_weight.shape[1]
    kv_part = kv_columns // parts
    qk_rows = qk_gains.shape[1]
    ends = [0]
    for columns in (head_width, head_width, ff_part, ff_part, ff_part, kv_part, GAIN_COLUMNS):
        ends.append(ends[-1] + columns)

    packed = pack_shards(
        norm_gains, qk_gains, q_weight, kv_weight, out_weight, gate_weight, up_weight, down_weight
    )
    gathered = gather_weights(packed).reshape(parts, width, ends[-1])
    halo = lax.ppermute(tokens, "tensor", [(i, i + 1) for i in range(parts - 1)])

    def piece(index):
        return [gathered[t, :, ends[index] : ends[index + 1]] for t in range(parts)]

    w_query, w_out, w_gate, w_up, w_down, w_kv = (piece(i) for i in range(6))
    w_keyval = jnp.concatenate(w_kv, axis=1)
    w_gains = gathered[0, :, ends[6] : ends[7]].astype(jnp.float32)
    gain_table = w_gains[:, :4].T
    qk_table = w_gains.reshape(-1, shard_rows, GAIN_COLUMNS)[:, :qk_rows, 4:6]
    qk_table = qk_table.reshape(head_width, 2).T

    own_input = tokens.astype(jnp.float32)
    both_input = jnp.concatenate([halo, tokens], axis=0).astype(jnp.float32)
    normed_both = norm_rows(both_input, gain_table[0]).astype(jnp.bfloat16)
    normed = normed_both[rows:]
    start = place * rows
    first = jnp.maximum(start - rows, 0)
    own_doc = lax.dynamic_slice_in_dim(segments, start, rows)
    halo_doc = jnp.where(place > 0, lax.dynamic_slice_in_dim(segments, first, rows), -1)
    both_doc = jnp.concatenate([halo_doc, own_doc])
    both_place = jnp.concatenate(
        [
            lax.dynamic_slice_in_dim(positions, first, rows),
            lax.dynamic_slice_in_dim(positions, start, rows),
        ]
    )
    half_width = head_width // 2
    frequency = ROPE_BASE ** (-jnp.arange(half_width, dtype=jnp.float32) * 2.0 / head_width)
    angles = both_place.astype(jnp.float32)[:, None] * frequency[None, :]
    cosine_both = jnp.cos(angles)
    sine_both = jnp.sin(angles)
    cosine_own, sine_own = cosine_both[rows:], sine_both[rows:]

    offsets = jnp.arange(rows)[:, None] + rows - jnp.arange(2 * rows)[None, :]
    allowed = (offsets >= 0) & (offsets < WINDOW) & (own_doc[:, None] == both_doc[None, :])
    score_scale = head_width ** (-0.5)

    keyval_raw = dot_plain(normed_both, w_keyval)
    key_raw = keyval_raw[:, :head_width]
    keys = rotate(norm_rows(key_raw, qk_table[1]), cosine_both, sine_both).astype(jnp.bfloat16)
    value_rows = keyval_raw[:, head_width:].astype(jnp.bfloat16)

    query_raw, queries, lse, context = [], [], [], []
    attn_own = None
    for t in range(parts):
        raw = dot_plain(normed, w_query[t])
        low = rotate(norm_rows(raw, qk_table[0]), cosine_own, sine_own).astype(jnp.bfloat16)
        masked = jnp.where(allowed, dot_last(low, keys) * score_scale, -1000000000.0)
        row_max = jnp.max(masked, axis=1, keepdims=True)
        exponent = jnp.exp(masked - row_max)
        row_total = jnp.sum(exponent, axis=1, keepdims=True)
        probabilities = (exponent / row_total).astype(jnp.bfloat16)
        mixed = dot_plain(probabilities, value_rows).astype(jnp.bfloat16)
        query_raw.append(raw)
        queries.append(low)
        lse.append(row_max + jnp.log(row_total))
        context.append(mixed)
        share = dot_last(mixed, w_out[t])
        attn_own = share if attn_own is None else attn_own + share

    residual = own_input + norm_rows(attn_own, gain_table[1])
    ffn_in = norm_rows(residual, gain_table[2]).astype(jnp.bfloat16)
    gate_pre, up_pre, hidden = [], [], []
    ffn_out = None
    for t in range(parts):
        gate_pre.append(dot_plain(ffn_in, w_gate[t]))
        up_pre.append(dot_plain(ffn_in, w_up[t]))
        hidden.append(geglu(gate_pre[t], up_pre[t]).astype(jnp.bfloat16))
        share = dot_last(hidden[t], w_down[t])
        ffn_out = share if ffn_out is None else ffn_out + share
    block_out = (residual + norm_rows(ffn_out, gain_table[3])).astype(jnp.bfloat16)
    top_grad = cotangent.astype(jnp.float32)
    ffn_grad_value, post_gain_rows = norm_back(ffn_out, gain_table[3], top_grad)
    ffn_grad = ffn_grad_value.astype(jnp.bfloat16)
    ffn_in_grad = None
    grads = [[] for _ in range(parts)]
    down_wgrad, gate_wgrad, up_wgrad = [], [], []
    for t in range(parts):
        hidden_grad = dot_plain(ffn_grad, w_down[t])
        gelu_back = jax.vjp(geglu, gate_pre[t], up_pre[t])[1]
        gate_grad_value, up_grad_value = gelu_back(hidden_grad)
        gate_grad = gate_grad_value.astype(jnp.bfloat16)
        up_grad = up_grad_value.astype(jnp.bfloat16)
        share = dot_last(gate_grad, w_gate[t]) + dot_last(up_grad, w_up[t])
        ffn_in_grad = share if ffn_in_grad is None else ffn_in_grad + share
        gate_wgrad.append(dot_first(ffn_in, gate_grad))
        up_wgrad.append(dot_first(ffn_in, up_grad))
        down_wgrad.append(dot_first(ffn_grad, hidden[t]))
    residual_part, pre_ffn_rows = norm_back(residual, gain_table[2], ffn_in_grad)
    residual_grad = top_grad + residual_part
    attn_grad_value, post_attn_rows = norm_back(attn_own, gain_table[1], residual_grad)
    attn_grad = attn_grad_value.astype(jnp.bfloat16)

    key_grad, value_grad, normed_grad = None, None, None
    query_gain_grad = None
    out_wgrad, query_wgrad = [], []
    for t in range(parts):
        context_grad = dot_plain(attn_grad, w_out[t]).astype(jnp.bfloat16)
        out_wgrad.append(dot_first(attn_grad, context[t]))
        masked = jnp.where(allowed, dot_last(queries[t], keys) * score_scale, -1000000000.0)
        probabilities = jnp.exp(masked - lse[t])
        prob_grad = dot_last(context_grad, value_rows)
        row_delta = jnp.sum(probabilities * prob_grad, axis=1, keepdims=True)
        score_grad = (probabilities * (prob_grad - row_delta) * score_scale).astype(jnp.bfloat16)
        query_grad = dot_plain(score_grad, keys)
        key_share = dot_first(score_grad, queries[t])
        value_share = dot_first(probabilities.astype(jnp.bfloat16), context_grad)
        key_grad = key_share if key_grad is None else key_grad + key_share
        value_grad = value_share if value_grad is None else value_grad + value_share
        unrotated = rotate(query_grad, cosine_own, -sine_own)
        raw_grad, gain_rows = norm_back(query_raw[t], qk_table[0], unrotated)
        gain_share = jnp.sum(gain_rows, axis=0)
        query_gain_grad = gain_share if query_gain_grad is None else query_gain_grad + gain_share
        raw_low = raw_grad.astype(jnp.bfloat16)
        share = dot_last(raw_low, w_query[t])
        normed_grad = share if normed_grad is None else normed_grad + share
        query_wgrad.append(dot_first(normed, raw_low))
    key_raw_grad, key_gain_rows = norm_back(
        key_raw, qk_table[1], rotate(key_grad, cosine_both, -sine_both)
    )
    keyval_low = jnp.concatenate([key_raw_grad, value_grad], axis=1).astype(jnp.bfloat16)
    next_part = lax.ppermute(
        keyval_low[:rows], "tensor", [(i + 1, i) for i in range(parts - 1)]
    )
    keyval_wgrad = dot_first(normed_both, keyval_low)
    keyval_own = (keyval_low[rows:].astype(jnp.float32) + next_part.astype(jnp.float32)).astype(
        jnp.bfloat16
    )
    normed_grad = normed_grad + dot_last(keyval_own, w_keyval)
    input_part, pre_attn_rows = norm_back(own_input, gain_table[0], normed_grad)
    tokens_grad = residual_grad + input_part

    gain_grads = jnp.stack(
        [
            jnp.sum(pre_attn_rows, axis=0),
            jnp.sum(post_attn_rows, axis=0),
            jnp.sum(pre_ffn_rows, axis=0),
            jnp.sum(post_gain_rows, axis=0),
        ],
        axis=1,
    )
    qk_grads = jnp.stack([query_gain_grad, jnp.sum(key_gain_rows, axis=0)], axis=1)
    qk_grads = jnp.pad(
        qk_grads.reshape(-1, qk_rows, 2), ((0, 0), (0, shard_rows - qk_rows), (0, 0))
    ).reshape(width, 2)
    gain_columns = jnp.concatenate(
        [gain_grads, qk_grads, jnp.zeros((width, GAIN_COLUMNS - 6), jnp.float32)], axis=1
    )
    blocks = []
    for t in range(parts):
        blocks.append(
            jnp.concatenate(
                [
                    value.astype(jnp.bfloat16)
                    for value in (
                        query_wgrad[t],
                        out_wgrad[t],
                        gate_wgrad[t],
                        up_wgrad[t],
                        down_wgrad[t],
                        keyval_wgrad[:, t * kv_part : (t + 1) * kv_part],
                        gain_columns if t == 0 else jnp.zeros_like(gain_columns),
                    )
                ],
                axis=1,
            )
        )
    reduced = reduce_grads(jnp.concatenate(blocks, axis=0))
    shared = lax.all_gather(reduced[:, ends[5] :], "tensor", axis=0)
    keyval_out = jnp.concatenate([shared[t, :, :kv_part] for t in range(parts)], axis=1)
    gain_out = shared[0, :, kv_part:]
    cut = [reduced[:, ends[i] : ends[i + 1]] for i in range(5)]
    return (
        block_out,
        tokens_grad,
        gain_out[:, :4].T,
        gain_out[:qk_rows, 4:6].T,
        cut[0],
        keyval_out,
        cut[1].T,
        cut[2],
        cut[3],
        cut[4].T,
    )


def solution(mesh):
    return jax.shard_map(
        per_device,
        mesh=mesh,
        in_specs=(
            P(("dp", "tensor"), None),
            P("dp"),
            P("dp"),
            P(None, "dp"),
            P(None, "dp"),
            P("dp", "tensor"),
            P("dp", None),
            P("tensor", "dp"),
            P("dp", "tensor"),
            P("dp", "tensor"),
            P("tensor", "dp"),
            P(("dp", "tensor"), None),
        ),
        out_specs=(
            P(("dp", "tensor"), None),
            P(("dp", "tensor"), None),
            P(None, "dp"),
            P(None, "dp"),
            P("dp", "tensor"),
            P("dp", None),
            P("tensor", "dp"),
            P("dp", "tensor"),
            P("dp", "tensor"),
            P("tensor", "dp"),
        ),
        check_vma=False,
    )
```

```python
import jax
import jax.numpy as jnp
from jax import lax
from jax.experimental import pallas as pl
from jax.experimental.pallas import tpu as pltpu
from jax.sharding import PartitionSpec as P

WINDOW = 512
GAIN_COLUMNS = 128


EPSILON = 1e-06
ROPE_BASE = 10000.0
GELU_SCALE = 0.7978845608028654


def norm_rows(values, gain_row):
    return (
        values * lax.rsqrt(jnp.mean(values * values, axis=-1, keepdims=True) + EPSILON) * gain_row
    )


def norm_back(values, gain_row, grad_out):
    inv_rms = lax.rsqrt(jnp.mean(values * values, axis=-1, keepdims=True) + EPSILON)
    weighted = grad_out * gain_row
    inner_mean = jnp.mean(values * weighted, axis=-1, keepdims=True)
    return (
        inv_rms * weighted - values * inv_rms * inv_rms * inv_rms * inner_mean,
        grad_out * values * inv_rms,
    )


def rotate(values, cosine_table, sine_table):
    half_width = values.shape[-1] // 2
    first_half = values[..., :half_width]
    second_half = values[..., half_width:]
    return jnp.concatenate(
        [
            first_half * cosine_table - second_half * sine_table,
            second_half * cosine_table + first_half * sine_table,
        ],
        axis=-1,
    )


def geglu(gate_pre, up_pre):
    inner_term = GELU_SCALE * (gate_pre + 0.044715 * gate_pre * gate_pre * gate_pre)
    return 0.5 * gate_pre * (1.0 + jnp.tanh(inner_term)) * up_pre


def dot_plain(left_side, right_side):
    return jnp.dot(left_side, right_side, preferred_element_type=jnp.float32)


def dot_last(left_side, right_side):
    return lax.dot_general(
        left_side, right_side, (((1,), (1,)), ((), ())), preferred_element_type=jnp.float32
    )


def dot_first(left_side, right_side):
    return lax.dot_general(
        left_side, right_side, (((0,), (0,)), ((), ())), preferred_element_type=jnp.float32
    )


def pack_shards(norm_gains, qk_gains, q_weight, kv_weight, out_weight, gate_weight, up_weight, down_weight):
    rows = q_weight.shape[0]
    kv_columns = kv_weight.shape[1] // lax.axis_size("tensor")
    kv_part = lax.dynamic_slice_in_dim(
        kv_weight, lax.axis_index("tensor") * kv_columns, kv_columns, axis=1
    )
    gain_part = jnp.concatenate(
        [
            norm_gains.T,
            jnp.pad(qk_gains.T, ((0, rows - qk_gains.shape[1]), (0, 0))),
            jnp.zeros((rows, GAIN_COLUMNS - 6), jnp.bfloat16),
        ],
        axis=1,
    )
    return jnp.concatenate(
        [q_weight, out_weight.T, gate_weight, up_weight, down_weight.T, kv_part, gain_part],
        axis=1,
    )


def gather_weights(packed):
    return lax.all_gather(packed, ("tensor", "dp"), axis=0, tiled=True)


def reduce_grads(grads):
    return lax.psum_scatter(
        grads, ("tensor", "dp"), scatter_dimension=0, tiled=True
    ).astype(jnp.float32)


def ffn_wgrads(ffn_in, ffn_grad, gate_grad, up_grad, hidden, parts):
    rows, width = ffn_in.shape
    columns = gate_grad.shape[1] // parts

    def body(in_ref, grad_ref, gate_ref, up_ref, hidden_ref, out_ref):
        out_ref[:, :columns] = dot_first(in_ref[...], gate_ref[...]).astype(jnp.bfloat16)
        out_ref[:, columns : 2 * columns] = dot_first(in_ref[...], up_ref[...]).astype(jnp.bfloat16)
        out_ref[:, 2 * columns :] = dot_first(grad_ref[...], hidden_ref[...]).astype(jnp.bfloat16)

    whole = pl.BlockSpec((rows, width), lambda t: (0, 0))
    slab = pl.BlockSpec((rows, columns), lambda t: (0, t))
    return pl.pallas_call(
        body,
        grid=(parts,),
        in_specs=[whole, whole, slab, slab, slab],
        out_specs=pl.BlockSpec((width, 3 * columns), lambda t: (t, 0)),
        out_shape=jax.ShapeDtypeStruct((parts * width, 3 * columns), jnp.bfloat16),
        compiler_params=pltpu.CompilerParams(vmem_limit_bytes=32 * 1024 * 1024),
        cost_estimate=pl.CostEstimate(
            flops=6 * rows * width * columns * parts,
            bytes_accessed=2 * parts * columns * 3 * (rows + width),
            transcendentals=0,
        ),
        name="ffn_wgrads",
    )(ffn_in, ffn_grad, gate_grad, up_grad, hidden)


def attn_wgrads(normed_both, attn_grad, query_low, context, keyval_low, gain_columns, parts):
    rows, width = attn_grad.shape
    columns = query_low.shape[1] // parts
    kv_part = keyval_low.shape[1] // parts

    def body(normed_ref, grad_ref, query_ref, context_ref, keyval_ref, gain_ref, out_ref):
        own = normed_ref[rows:, :]
        out_ref[:, :columns] = dot_first(own, query_ref[...]).astype(jnp.bfloat16)
        out_ref[:, columns : 2 * columns] = dot_first(grad_ref[...], context_ref[...]).astype(
            jnp.bfloat16
        )
        out_ref[:, 2 * columns : 2 * columns + kv_part] = dot_first(
            normed_ref[...], keyval_ref[...]
        ).astype(jnp.bfloat16)
        out_ref[:, 2 * columns + kv_part :] = gain_ref[...].astype(jnp.bfloat16)

    slab = pl.BlockSpec((rows, columns), lambda t: (0, t))
    total = 2 * columns + kv_part + gain_columns.shape[1]
    return pl.pallas_call(
        body,
        grid=(parts,),
        in_specs=[
            pl.BlockSpec(normed_both.shape, lambda t: (0, 0)),
            pl.BlockSpec((rows, width), lambda t: (0, 0)),
            slab,
            slab,
            pl.BlockSpec((keyval_low.shape[0], kv_part), lambda t: (0, t)),
            pl.BlockSpec(gain_columns.shape, lambda t: (0, 0)),
        ],
        out_specs=pl.BlockSpec((width, total), lambda t: (t, 0)),
        out_shape=jax.ShapeDtypeStruct((parts * width, total), jnp.bfloat16),
        compiler_params=pltpu.CompilerParams(vmem_limit_bytes=32 * 1024 * 1024),
        cost_estimate=pl.CostEstimate(
            flops=2 * rows * width * (2 * columns + 2 * kv_part) * parts,
            bytes_accessed=2 * parts * total * (rows + width),
            transcendentals=0,
        ),
        name="attn_wgrads",
    )(normed_both, attn_grad, query_low, context, keyval_low, gain_columns)


def per_device(
    tokens,
    segments,
    positions,
    norm_gains,
    qk_gains,
    q_weight,
    kv_weight,
    out_weight,
    gate_weight,
    up_weight,
    down_weight,
    cotangent,
):
    parts = lax.axis_size("tensor")
    place = lax.axis_index("tensor")
    rows, width = tokens.shape
    shard_rows = q_weight.shape[0]
    head_width = q_weight.shape[1]
    ff_part = gate_weight.shape[1]
    kv_columns = kv_weight.shape[1]
    kv_part = kv_columns // parts
    qk_rows = qk_gains.shape[1]
    ends = [0]
    for columns in (head_width, head_width, ff_part, ff_part, ff_part, kv_part, GAIN_COLUMNS):
        ends.append(ends[-1] + columns)

    packed = pack_shards(
        norm_gains, qk_gains, q_weight, kv_weight, out_weight, gate_weight, up_weight, down_weight
    )
    gathered = gather_weights(packed).reshape(parts, width, ends[-1])
    halo = lax.ppermute(tokens, "tensor", [(i, i + 1) for i in range(parts - 1)])

    def piece(index):
        return [gathered[t, :, ends[index] : ends[index + 1]] for t in range(parts)]

    w_query, w_out, w_gate, w_up, w_down, w_kv = (piece(i) for i in range(6))
    w_keyval = jnp.concatenate(w_kv, axis=1)
    w_gains = gathered[0, :, ends[6] : ends[7]].astype(jnp.float32)
    gain_table = w_gains[:, :4].T
    qk_table = w_gains.reshape(-1, shard_rows, GAIN_COLUMNS)[:, :qk_rows, 4:6]
    qk_table = qk_table.reshape(head_width, 2).T

    own_input = tokens.astype(jnp.float32)
    both_input = jnp.concatenate([halo, tokens], axis=0).astype(jnp.float32)
    normed_both = norm_rows(both_input, gain_table[0]).astype(jnp.bfloat16)
    normed = normed_both[rows:]
    start = place * rows
    first = jnp.maximum(start - rows, 0)
    own_doc = lax.dynamic_slice_in_dim(segments, start, rows)
    halo_doc = jnp.where(place > 0, lax.dynamic_slice_in_dim(segments, first, rows), -1)
    both_doc = jnp.concatenate([halo_doc, own_doc])
    both_place = jnp.concatenate(
        [
            lax.dynamic_slice_in_dim(positions, first, rows),
            lax.dynamic_slice_in_dim(positions, start, rows),
        ]
    )
    half_width = head_width // 2
    frequency = ROPE_BASE ** (-jnp.arange(half_width, dtype=jnp.float32) * 2.0 / head_width)
    angles = both_place.astype(jnp.float32)[:, None] * frequency[None, :]
    cosine_both = jnp.cos(angles)
    sine_both = jnp.sin(angles)
    cosine_own, sine_own = cosine_both[rows:], sine_both[rows:]

    offsets = jnp.arange(rows)[:, None] + rows - jnp.arange(2 * rows)[None, :]
    allowed = (offsets >= 0) & (offsets < WINDOW) & (own_doc[:, None] == both_doc[None, :])
    score_scale = head_width ** (-0.5)

    keyval_raw = dot_plain(normed_both, w_keyval)
    key_raw = keyval_raw[:, :head_width]
    keys = rotate(norm_rows(key_raw, qk_table[1]), cosine_both, sine_both).astype(jnp.bfloat16)
    value_rows = keyval_raw[:, head_width:].astype(jnp.bfloat16)

    query_raw, queries, lse, context = [], [], [], []
    attn_own = None
    for t in range(parts):
        raw = dot_plain(normed, w_query[t])
        low = rotate(norm_rows(raw, qk_table[0]), cosine_own, sine_own).astype(jnp.bfloat16)
        masked = jnp.where(allowed, dot_last(low, keys) * score_scale, -1000000000.0)
        row_max = jnp.max(masked, axis=1, keepdims=True)
        exponent = jnp.exp(masked - row_max)
        row_total = jnp.sum(exponent, axis=1, keepdims=True)
        probabilities = (exponent / row_total).astype(jnp.bfloat16)
        mixed = dot_plain(probabilities, value_rows).astype(jnp.bfloat16)
        query_raw.append(raw)
        queries.append(low)
        lse.append(row_max + jnp.log(row_total))
        context.append(mixed)
        share = dot_last(mixed, w_out[t])
        attn_own = share if attn_own is None else attn_own + share

    residual = own_input + norm_rows(attn_own, gain_table[1])
    ffn_in = norm_rows(residual, gain_table[2]).astype(jnp.bfloat16)
    gate_pre, up_pre, hidden = [], [], []
    ffn_out = None
    for t in range(parts):
        gate_pre.append(dot_plain(ffn_in, w_gate[t]))
        up_pre.append(dot_plain(ffn_in, w_up[t]))
        hidden.append(geglu(gate_pre[t], up_pre[t]).astype(jnp.bfloat16))
        share = dot_last(hidden[t], w_down[t])
        ffn_out = share if ffn_out is None else ffn_out + share
    block_out = (residual + norm_rows(ffn_out, gain_table[3])).astype(jnp.bfloat16)
    top_grad = cotangent.astype(jnp.float32)
    ffn_grad_value, post_gain_rows = norm_back(ffn_out, gain_table[3], top_grad)
    ffn_grad = ffn_grad_value.astype(jnp.bfloat16)
    ffn_in_grad = None
    gate_grads, up_grads = [], []
    for t in range(parts):
        hidden_grad = dot_plain(ffn_grad, w_down[t])
        gelu_back = jax.vjp(geglu, gate_pre[t], up_pre[t])[1]
        gate_grad_value, up_grad_value = gelu_back(hidden_grad)
        gate_grad = gate_grad_value.astype(jnp.bfloat16)
        up_grad = up_grad_value.astype(jnp.bfloat16)
        share = dot_last(gate_grad, w_gate[t]) + dot_last(up_grad, w_up[t])
        ffn_in_grad = share if ffn_in_grad is None else ffn_in_grad + share
        gate_grads.append(gate_grad)
        up_grads.append(up_grad)
    ffn_local = ffn_wgrads(
        ffn_in,
        ffn_grad,
        *(jnp.concatenate(group, axis=1) for group in (gate_grads, up_grads, hidden)),
        parts,
    )
    residual_part, pre_ffn_rows = norm_back(residual, gain_table[2], ffn_in_grad)
    residual_grad = top_grad + residual_part
    attn_grad_value, post_attn_rows = norm_back(attn_own, gain_table[1], residual_grad)
    attn_grad = attn_grad_value.astype(jnp.bfloat16)
    attn_grad, ffn_local = lax.optimization_barrier((attn_grad, ffn_local))
    ffn_reduced = reduce_grads(ffn_local)

    key_grad, value_grad, normed_grad = None, None, None
    query_gain_grad = None
    raw_lows = []
    for t in range(parts):
        context_grad = dot_plain(attn_grad, w_out[t]).astype(jnp.bfloat16)
        masked = jnp.where(allowed, dot_last(queries[t], keys) * score_scale, -1000000000.0)
        probabilities = jnp.exp(masked - lse[t])
        prob_grad = dot_last(context_grad, value_rows)
        row_delta = jnp.sum(probabilities * prob_grad, axis=1, keepdims=True)
        score_grad = (probabilities * (prob_grad - row_delta) * score_scale).astype(jnp.bfloat16)
        query_grad = dot_plain(score_grad, keys)
        key_share = dot_first(score_grad, queries[t])
        value_share = dot_first(probabilities.astype(jnp.bfloat16), context_grad)
        key_grad = key_share if key_grad is None else key_grad + key_share
        value_grad = value_share if value_grad is None else value_grad + value_share
        unrotated = rotate(query_grad, cosine_own, -sine_own)
        raw_grad, gain_rows = norm_back(query_raw[t], qk_table[0], unrotated)
        gain_share = jnp.sum(gain_rows, axis=0)
        query_gain_grad = gain_share if query_gain_grad is None else query_gain_grad + gain_share
        raw_low = raw_grad.astype(jnp.bfloat16)
        share = dot_last(raw_low, w_query[t])
        normed_grad = share if normed_grad is None else normed_grad + share
        raw_lows.append(raw_low)
    key_raw_grad, key_gain_rows = norm_back(
        key_raw, qk_table[1], rotate(key_grad, cosine_both, -sine_both)
    )
    keyval_low = jnp.concatenate([key_raw_grad, value_grad], axis=1).astype(jnp.bfloat16)
    next_part = lax.ppermute(
        keyval_low[:rows], "tensor", [(i + 1, i) for i in range(parts - 1)]
    )
    keyval_own = (keyval_low[rows:].astype(jnp.float32) + next_part.astype(jnp.float32)).astype(
        jnp.bfloat16
    )
    normed_grad = normed_grad + dot_last(keyval_own, w_keyval)
    input_part, pre_attn_rows = norm_back(own_input, gain_table[0], normed_grad)
    tokens_grad = residual_grad + input_part

    gain_grads = jnp.stack(
        [
            jnp.sum(pre_attn_rows, axis=0),
            jnp.sum(post_attn_rows, axis=0),
            jnp.sum(pre_ffn_rows, axis=0),
            jnp.sum(post_gain_rows, axis=0),
        ],
        axis=1,
    )
    qk_grads = jnp.stack([query_gain_grad, jnp.sum(key_gain_rows, axis=0)], axis=1)
    qk_grads = jnp.pad(
        qk_grads.reshape(-1, qk_rows, 2), ((0, 0), (0, shard_rows - qk_rows), (0, 0))
    ).reshape(width, 2)
    gain_columns = jnp.concatenate(
        [gain_grads, qk_grads, jnp.zeros((width, GAIN_COLUMNS - 6), jnp.float32)], axis=1
    )
    attn_local = attn_wgrads(
        normed_both,
        attn_grad,
        jnp.concatenate(raw_lows, axis=1),
        jnp.concatenate(context, axis=1),
        keyval_low,
        gain_columns,
        parts,
    )
    attn_local, ffn_reduced = lax.optimization_barrier((attn_local, ffn_reduced))
    attn_reduced = reduce_grads(attn_local)
    shared = lax.all_gather(attn_reduced[:, 2 * head_width :], "tensor", axis=0)
    keyval_out = jnp.concatenate([shared[t, :, :kv_part] for t in range(parts)], axis=1)
    gain_out = shared[0, :, kv_part:]
    return (
        block_out,
        tokens_grad,
        gain_out[:, :4].T,
        gain_out[:qk_rows, 4:6].T,
        attn_reduced[:, :head_width],
        keyval_out,
        attn_reduced[:, head_width : 2 * head_width].T,
        ffn_reduced[:, :ff_part],
        ffn_reduced[:, ff_part : 2 * ff_part],
        ffn_reduced[:, 2 * ff_part :].T,
    )


def solution(mesh):
    return jax.shard_map(
        per_device,
        mesh=mesh,
        in_specs=(
            P(("dp", "tensor"), None),
            P("dp"),
            P("dp"),
            P(None, "dp"),
            P(None, "dp"),
            P("dp", "tensor"),
            P("dp", None),
            P("tensor", "dp"),
            P("dp", "tensor"),
            P("dp", "tensor"),
            P("tensor", "dp"),
            P(("dp", "tensor"), None),
        ),
        out_specs=(
            P(("dp", "tensor"), None),
            P(("dp", "tensor"), None),
            P(None, "dp"),
            P(None, "dp"),
            P("dp", "tensor"),
            P("dp", None),
            P("tensor", "dp"),
            P("dp", "tensor"),
            P("dp", "tensor"),
            P("tensor", "dp"),
        ),
        check_vma=False,
    )
```
